32 devices in a mesh: expert: 16 (over z, y, x), tensor: 2 (over core).
Axes of the slice: x: 2, y: 2, z: 4, core: 2. Of those that a mesh axis runs over, the one named last changes fastest.
Arguments:
- context: bfloat16 [1024, 4096], P('expert', 'tensor'), may hold values from -6 to 6
- output_weight: bfloat16 [4096, 2048], P('tensor'), may hold values from -0.09375 to 0.09375
- residual: bfloat16 [1024, 2048], P('expert'), may hold values from -6 to 6
- norm_gain: float32 [2048], replicated, may hold values from 0.5 to 1.5
- routes: int32 [1024, 8], P('expert'), may hold values from 0 to 15, all different within a row; in each aligned block of 64 rows (0 to 63, 64 to 127, ...) at most 40 rows name the same one
- gate_values: float32 [1024, 8], P('expert'), may hold values from 0.05 to 0.25
- gate_weight: bfloat16 [2048, 12288], P(None, ('expert', 'tensor')), may hold values from -0.125 to 0.125
- up_weight: bfloat16 [2048, 12288], P(None, ('expert', 'tensor')), may hold values from -0.125 to 0.125
- down_weight: bfloat16 [12288, 2048], P(('expert', 'tensor')), may hold values from -0.21875 to 0.21875
Outputs:
- layer_out: bfloat16 [1024, 2048], P(('expert', 'tensor'))
The draws below stay inside these ranges and needn't reach their ends.
Inputs may be any that keep to these rules, and one draw needn't show every extreme that they name: `routes`: in each aligned block of 64 rows (the tokens of one index of expert), no expert is named by more than 40 rows, a bound that some block reaches.
All inputs are finite; a program needn't handle non-finite values.
Results may differ from the reference program's by a relative error of at most 0.014.
Values may be sent and summed in bfloat16 or wider, within the bound.
No kernel may reach another device: no remote copies, remote signals or barrier semaphores. Data moves between devices by JAX's collectives and lax.ppermute only.
A program may use at most 64 MiB of HBM per device.

```python
import math
import jax
import jax.numpy as jnp
import numpy as np
from jax import lax

D = 2048
HQ = 32
HD = 128
FFE = 768
TOPK = 8
HALVES = 2
TOK_GRP = 64
TOKENS = 1024
EXP_IDX = 1
EXPERTS = 16
CAP = 40
N_EXPERT = 16
N_TENSOR = 2


def block_levels(own_key, shape, pieces, low, high):
    level = 1.0
    for dim, parts in pieces:
        steps = jax.random.uniform(jax.random.fold_in(jax.random.fold_in(own_key, 6), dim), (parts,), jnp.float32, low / len(pieces), high / len(pieces))
        level = level * jnp.repeat(jnp.exp(steps), shape[dim] // parts).reshape((-1,) + (1,) * (len(shape) - 1 - dim))
    return level


def shared_out(key, own, number, rows, amount, top, bound, skew):
    order = jax.random.permutation(key, amount)
    heavy_load, usual = shares(amount, rows * top, bound, skew, True), shares(amount, rows * top, bound, skew, False)
    places = jnp.arange(amount)

    def named(sizes, turn):
        used = int((sizes > 0).sum())
        fixed = max(1, used // 4)
        passed = fixed + (places - fixed + turn * (used - fixed)) % max(1, amount - fixed)
        return jnp.zeros((amount,), jnp.int32).at[order[jnp.where(places < fixed, places, passed)]].set(jnp.asarray(sizes, jnp.int32))

    sizes = jnp.where(number % 4 == 0, named(heavy_load, number // 4), named(usual, number - number // 4 - 1))
    mixed = jax.random.permutation(jax.random.fold_in(own, 3), amount)
    giver, receiver = mixed[0:amount // 2 * 2:2], mixed[1:amount // 2 * 2:2]
    slack = jnp.minimum(sizes[giver] - 1, bound - sizes[receiver]) // 2
    slack = jnp.where((giver == order[0]) | (receiver == order[0]) | (sizes[receiver] == 0), 0, jnp.maximum(slack, 0))
    passed = jax.random.randint(jax.random.fold_in(own, 4), (amount // 2,), 0, 1 << 20) % (slack + 1)
    sizes = sizes.at[giver].add(-passed).at[receiver].add(passed)
    items = jnp.searchsorted(jnp.cumsum(sizes), jnp.arange(rows * top), side="right").astype(jnp.int32)
    listing = items.reshape(top, rows).T
    listing = listing[jax.random.permutation(jax.random.fold_in(own, 1), rows)]
    turn = jax.random.randint(jax.random.fold_in(own, 2), (rows, 1), 0, top)
    return jnp.take_along_axis(listing, (jnp.arange(top)[None, :] + turn) % top, axis=1)


def shares(count, total, most, lean, full):
    weights = [(1 << 20) // math.isqrt(rank ** lean) + 1 for rank in range(1, count + 1)]
    largest = most if full else min(most, max(-(-total // count), total * weights[0] // sum(weights)))
    least = 1 if total - largest >= count - 1 else 0
    holding, spare = [largest] + [least] * (count - 1), total - largest - least * (count - 1)
    while spare > 0:
        movable = [i for i in range(1, count) if holding[i] < largest] or [i for i in range(1, count) if holding[i] < most]
        pool, left = sum([weights[i] for i in movable]), spare
        for i in movable:
            addition = min(most - holding[i], max(1, left * weights[i] // pool), spare)
            holding[i] = holding[i] + addition
            spare = spare - addition
    return np.array(holding)


def centred(stream_key, extent, width, limit, shards=(), held_as=jnp.bfloat16):
    level = block_levels(stream_key, extent, shards, -0.22, 0.18) if shards else 1.0
    drawn = jax.random.normal(stream_key, extent, jnp.float32) * width * level
    return jnp.minimum(jnp.maximum(drawn, -limit), limit).astype(held_as)


def setup_inputs(seed: int = 0) -> dict:
    splits = jax.random.split(jax.random.key(seed), 10)
    context = centred(splits[0], (TOKENS, HQ * HD), 1.0, 6.0, ((0, 16), (1, 2)))
    output_weight = centred(splits[1], (HQ * HD, D), (HQ * HD) ** -0.5, 0.09375, ((0, 2),))
    residual = centred(splits[2], (TOKENS, D), 1.0, 6.0, ((0, 16),))
    norm_gain = jnp.clip(1.0 + 0.1 * jax.random.normal(splits[3], (D,), jnp.float32), 0.5, 1.5)
    routes_keys = jax.random.split(jax.random.fold_in(splits[4], 1), TOKENS // TOK_GRP)
    routes_turns = jax.random.permutation(jax.random.fold_in(splits[4], 3), TOKENS // TOK_GRP)
    routes = jax.vmap(lambda own, number: shared_out(jax.random.fold_in(splits[4], 2), own, number, TOK_GRP, EXPERTS, TOPK, CAP, 2))(routes_keys, routes_turns).reshape((TOKENS, TOPK))
    gate_values = jnp.clip(0.05 + 0.2 * jax.random.uniform(splits[5], (TOKENS, TOPK), jnp.float32) ** block_levels(splits[5], (TOKENS, TOPK), ((0, 16),), -0.2, 0.2), 0.05, 0.25)
    gate_weight = centred(splits[6], (D, EXPERTS * FFE), D ** -0.5, 0.125, ((1, 32),))
    up_weight = centred(splits[7], (D, EXPERTS * FFE), D ** -0.5, 0.125, ((1, 32),))
    down_weight = centred(splits[8], (EXPERTS * FFE, D), FFE ** -0.5, 0.21875, ((0, 32),))
    return dict(context=context, output_weight=output_weight, residual=residual, norm_gain=norm_gain, routes=routes, gate_values=gate_values, gate_weight=gate_weight, up_weight=up_weight, down_weight=down_weight)


def root_norm(values, norm_gain):
    squares = values * values
    inverse = lax.rsqrt(lax.optimization_barrier(jnp.mean(squares, axis=-1, keepdims=True)) + 1e-06)
    return (values * inverse * norm_gain).astype(jnp.bfloat16)

def reference(context, output_weight, residual, norm_gain, routes, gate_values, gate_weight, up_weight, down_weight):
    head_part = HQ * HD // N_TENSOR
    half_width = FFE // HALVES
    gate_experts = gate_weight.reshape(D, EXPERTS, FFE).transpose(1, 0, 2)
    up_experts = up_weight.reshape(D, EXPERTS, FFE).transpose(1, 0, 2)
    down_experts = down_weight.reshape(EXPERTS, FFE, D)
    parts_weight = output_weight.reshape(N_TENSOR, head_part, D)

    def one_group(inputs):
        group_context, group_residual, group_routes, group_gates = inputs
        head_total = jnp.zeros((TOK_GRP, D), jnp.float32)
        for part_index in range(N_TENSOR):
            head_piece = group_context[:, part_index * head_part:(part_index + 1) * head_part]
            rounded = jnp.dot(head_piece, parts_weight[part_index], preferred_element_type=jnp.float32).astype(jnp.bfloat16)
            rounded = lax.optimization_barrier(rounded)
            head_total = head_total + rounded.astype(jnp.float32)
        attention = (group_residual.astype(jnp.float32) + head_total).astype(jnp.bfloat16)
        normed = root_norm(attention.astype(jnp.float32), norm_gain)
        expert_ids = jnp.arange(EXPERTS, dtype=jnp.int32)
        expert_hits = lax.optimization_barrier(jnp.sum((group_routes[:, :, None] == expert_ids[None, None, :]).astype(jnp.int32), axis=1))
        rank_table = jnp.cumsum(expert_hits, axis=0) - expert_hits
        slot_index = jnp.take_along_axis(rank_table, group_routes, axis=1).astype(jnp.int32)
        token_ids = jnp.broadcast_to(jnp.arange(TOK_GRP, dtype=jnp.int32)[:, None], group_routes.shape)
        token_table = jnp.full((EXPERTS, CAP), TOK_GRP, jnp.int32).at[group_routes, slot_index].set(token_ids)
        padded = jnp.concatenate([normed, jnp.zeros((1, D), jnp.bfloat16)], axis=0)

        def one_expert(expert_inputs):
            rows_index, gate_block, up_block, down_block = expert_inputs
            slot_rows = jnp.take(padded, rows_index, axis=0)
            halves = []
            for half_index in range(HALVES):
                column_start = half_index * half_width
                gate_out = jnp.dot(slot_rows, gate_block[:, column_start:column_start + half_width], preferred_element_type=jnp.float32)
                up_out = jnp.dot(slot_rows, up_block[:, column_start:column_start + half_width], preferred_element_type=jnp.float32)
                activated = (jax.nn.silu(gate_out) * up_out).astype(jnp.bfloat16)
                halves.append(jnp.dot(activated, down_block[column_start:column_start + half_width], preferred_element_type=jnp.float32).astype(jnp.bfloat16))
            return jnp.stack(halves, axis=1)
        expert_out = lax.map(one_expert, (token_table, gate_experts, up_experts, down_experts))
        flat_out = expert_out.reshape(EXPERTS * CAP, HALVES, D)
        picked = jnp.take(flat_out, group_routes * CAP + slot_index, axis=0).astype(jnp.float32)
        class_base = group_routes % EXP_IDX * HALVES
        expert_sum = jnp.zeros((TOK_GRP, D), jnp.float32)
        for class_index in range(N_TENSOR):
            weights = jnp.stack([jnp.where(class_base + half_index == class_index, group_gates, jnp.zeros_like(group_gates)) for half_index in range(HALVES)], axis=2)
            class_term = jnp.einsum('gkh,gkhd->gd', weights, picked, precision=lax.Precision.HIGHEST).astype(jnp.bfloat16)
            class_term = lax.optimization_barrier(class_term)
            expert_sum = expert_sum + class_term.astype(jnp.float32)
        return (attention.astype(jnp.float32) + expert_sum).astype(jnp.bfloat16)
    layer_rows = lax.map(one_group, (context.reshape(N_EXPERT, TOK_GRP, HQ * HD), residual.reshape(N_EXPERT, TOK_GRP, D), routes.reshape(N_EXPERT, TOK_GRP, TOPK), gate_values.reshape(N_EXPERT, TOK_GRP, TOPK)))
    return layer_rows.reshape(N_EXPERT * TOK_GRP, D)
```

```python
import functools

import jax
import jax.numpy as jnp
from jax import lax
from jax.experimental import pallas as pl
from jax.experimental.pallas import tpu as pltpu
from jax.sharding import PartitionSpec as P

HALVES = 2
PLANE = 4
LANES = 128
AXES = ("expert", "tensor")
VMEM = pl.BlockSpec(memory_space=pltpu.VMEM)
KERNEL_VMEM = 12 * 1024 * 1024


def head_kernel(context_ref, weight_ref, mine_ref, other_ref, buffer, sems):
    steps = sems.shape[0]
    depth = weight_ref.shape[0] // steps
    copies = [
        pltpu.make_async_copy(
            weight_ref.at[pl.ds(i * depth, depth), :],
            buffer.at[pl.ds(i * depth, depth), :],
            sems.at[i],
        )
        for i in range(steps)
    ]
    for copy in copies:
        copy.start()
    total = None
    for i, copy in enumerate(copies):
        copy.wait()
        part = jnp.dot(
            context_ref[:, i * depth : (i + 1) * depth],
            buffer[i * depth : (i + 1) * depth, :],
            preferred_element_type=jnp.float32,
        )
        total = part if total is None else total + part
    rows = mine_ref.shape[0]
    low, high = total[:rows].astype(jnp.bfloat16), total[rows:].astype(jnp.bfloat16)
    first = lax.axis_index("tensor") == 0
    mine_ref[...] = jnp.where(first, low, high)
    other_ref[...] = jnp.where(first, high, low)


def head_parts(context, output_weight):
    rows = context.shape[0] // 2
    width = output_weight.shape[1]
    part = jax.ShapeDtypeStruct((rows, width), jnp.bfloat16)
    steps = 8
    return pl.pallas_call(
        head_kernel,
        out_shape=(part, part),
        in_specs=[VMEM, pl.BlockSpec(memory_space=pltpu.HBM)],
        out_specs=(VMEM, VMEM),
        scratch_shapes=[
            pltpu.VMEM(output_weight.shape, jnp.bfloat16),
            pltpu.SemaphoreType.DMA((steps,)),
        ],
        compiler_params=pltpu.CompilerParams(vmem_limit_bytes=2 * KERNEL_VMEM),
        cost_estimate=pl.CostEstimate(
            flops=2 * context.size * width,
            bytes_accessed=output_weight.size * 2,
            transcendentals=0,
        ),
        name="head_parts",
    )(context, pltpu.with_memory_space_constraint(output_weight, pltpu.HBM))


def norm_kernel(
    experts, mine_ref, theirs_ref, residual_ref, gain_ref, routes_ref, gates_ref,
    attention_ref, block_ref,
):
    rows, width = mine_ref.shape
    start = pl.multiple_of(lax.axis_index("tensor") * rows, rows)
    head = mine_ref[...].astype(jnp.float32) + theirs_ref[...].astype(jnp.float32)
    residual = residual_ref[pl.ds(start, rows), :].astype(jnp.float32)
    attention = (residual + head).astype(jnp.bfloat16)
    attention_ref[...] = attention
    values = attention.astype(jnp.float32)
    inverse = lax.rsqrt(jnp.mean(values * values, axis=-1, keepdims=True) + 1e-06)
    block_ref[:, :width] = (values * inverse * gain_ref[...]).astype(jnp.bfloat16)
    lanes = block_ref.shape[1] - width
    lane = lax.broadcasted_iota(jnp.int32, (rows, lanes), 1)
    owner = jnp.where(lane < experts, lane, lane - experts)
    routes = routes_ref[pl.ds(start, rows), :]
    gates = gates_ref[pl.ds(start, rows), :]
    table = jnp.zeros((rows, lanes), jnp.float32)
    for k in range(routes.shape[1]):
        table = jnp.where(routes[:, k : k + 1] == owner, gates[:, k : k + 1], table)
    coarse = table.astype(jnp.bfloat16).astype(jnp.float32)
    table = jnp.where(lane < experts, coarse, table - coarse)
    block_ref[:, width:] = jnp.where(lane < 2 * experts, table, 0.0).astype(jnp.bfloat16)


def norm_block(experts, mine, theirs, residual, norm_gain, routes, gate_values):
    rows, width = mine.shape
    lanes = -(-2 * experts // LANES) * LANES
    return pl.pallas_call(
        functools.partial(norm_kernel, experts),
        out_shape=(
            jax.ShapeDtypeStruct((rows, width), jnp.bfloat16),
            jax.ShapeDtypeStruct((rows, width + lanes), jnp.bfloat16),
        ),
        in_specs=[VMEM] * 6,
        out_specs=(VMEM, VMEM),
        compiler_params=pltpu.CompilerParams(vmem_limit_bytes=KERNEL_VMEM),
        cost_estimate=pl.CostEstimate(
            flops=8 * mine.size, bytes_accessed=mine.size * 12, transcendentals=0
        ),
        name="norm_block",
    )(mine, theirs, residual, norm_gain.reshape(1, -1), routes, gate_values)


def expert_kernel(
    experts, near_ref, far_ref, gate_own_ref, gate_other_ref, up_own_ref, up_other_ref,
    down_own_ref, down_other_ref, keep_ref, send_ref,
):
    width = gate_own_ref.shape[0]
    blocks = jnp.concatenate([near_ref[...], far_ref[...]], axis=0)
    table = blocks[:, width:].astype(jnp.float32)
    lane = lax.broadcasted_iota(jnp.int32, table.shape, 1)
    me = lax.axis_index("expert")
    chosen = (lane == me) | (lane == me + experts)
    weight = jnp.sum(jnp.where(chosen, table, 0.0), axis=1, keepdims=True)
    rows = blocks[:, :width]

    def hidden(gate_ref, up_ref):
        gate = jnp.dot(rows, gate_ref[...], preferred_element_type=jnp.float32)
        up = jnp.dot(rows, up_ref[...], preferred_element_type=jnp.float32)
        return (jax.nn.silu(gate) * up * weight).astype(jnp.bfloat16)

    own, other = hidden(gate_own_ref, up_own_ref), hidden(gate_other_ref, up_other_ref)
    near_rows = near_ref.shape[0]
    step = 4 * LANES
    for j in range(width // step):
        cols = slice(j * step, (j + 1) * step)
        out = jnp.dot(own, down_own_ref[:, cols], preferred_element_type=jnp.float32)
        out += jnp.dot(other, down_other_ref[:, cols], preferred_element_type=jnp.float32)
        out = out.astype(jnp.bfloat16)
        keep_ref[:, cols] = out[:near_rows]
        send_ref[:, cols] = out[near_rows:]


def expert_rows(experts, near, far, weights):
    width = weights[0].shape[0]
    rows = near.shape[0] + far.shape[0]
    flops = 2 * rows * sum(w.size for w in weights)
    return pl.pallas_call(
        functools.partial(expert_kernel, experts),
        out_shape=tuple(
            jax.ShapeDtypeStruct((a.shape[0], width), jnp.bfloat16) for a in (near, far)
        ),
        in_specs=[VMEM] * (2 + len(weights)),
        out_specs=(VMEM, VMEM),
        compiler_params=pltpu.CompilerParams(vmem_limit_bytes=KERNEL_VMEM),
        cost_estimate=pl.CostEstimate(
            flops=flops, bytes_accessed=rows * width * 8, transcendentals=rows * width
        ),
        name="expert_rows",
    )(near, far, *weights)


def device_moves(expert_count, tensor_count, target):
    return [
        (e * tensor_count + t, f * tensor_count + u)
        for e in range(expert_count)
        for t in range(tensor_count)
        for f, u in [target(e, t)]
    ]


def dense_local(
    context, output_weight, residual, norm_gain, routes, gate_values, gate_weight, up_weight,
    down_weight,
):
    expert_count, tensor_count = lax.axis_size("expert"), lax.axis_size("tensor")
    layers = expert_count // PLANE
    rows = context.shape[0] // tensor_count

    def move(values, target):
        return lax.ppermute(values, AXES, device_moves(expert_count, tensor_count, target))

    def across(values):
        return move(values, lambda e, t: (e, 1 - t))

    def side(values):
        return move(values, lambda e, t: (e ^ (1 + t), t))

    def cross(values):
        return move(values, lambda e, t: (e ^ (2 - t), t))

    def along(values, hops):
        return move(values, lambda e, t: ((e + hops * PLANE) % expert_count, t))

    mine, other = head_parts(context, output_weight)
    theirs = across(other)
    shares, _ = lax.optimization_barrier(((gate_weight, up_weight, down_weight), other))
    weights = [w for share in shares for w in (share, across(share))]
    attention, block = norm_block(
        expert_count, mine, theirs, residual, norm_gain, routes, gate_values
    )
    total = attention.astype(jnp.float32)
    layer_blocks = [block if k == 0 else along(block, k) for k in range(layers)]
    for k, layer in enumerate(layer_blocks):
        near = jnp.concatenate([layer, side(layer)], axis=0)
        far = cross(near)
        keep, send = expert_rows(expert_count, near, far, weights)
        kept = keep.astype(jnp.float32) + cross(send).astype(jnp.float32)
        mine_sum = kept[:rows] + side(kept[rows:].astype(jnp.bfloat16)).astype(jnp.float32)
        if k:
            mine_sum = along(mine_sum.astype(jnp.bfloat16), -k).astype(jnp.float32)
        total = total + mine_sum
    return total.astype(jnp.bfloat16)


def root_norm(values, norm_gain):
    squares = values * values
    inverse = lax.rsqrt(jnp.mean(squares, axis=-1, keepdims=True) + 1e-06)
    return (values * inverse * norm_gain).astype(jnp.bfloat16)


def routed_local(
    context,
    output_weight,
    residual,
    norm_gain,
    routes,
    gate_values,
    gate_weight,
    up_weight,
    down_weight,
):
    tensor_count = lax.axis_size("tensor")
    expert_count = lax.axis_size("expert")
    tensor_index = lax.axis_index("tensor")
    group_rows = context.shape[0]
    token_rows = group_rows // tensor_count
    model_width = residual.shape[1]
    per_owner = tensor_count // HALVES
    experts_total = expert_count * per_owner
    capacity = 2 * (group_rows * routes.shape[1] * 5 // (8 * experts_total))
    local_expert = tensor_index // HALVES
    head_part = jnp.dot(context, output_weight, preferred_element_type=jnp.float32)
    head_total = lax.psum(head_part.astype(jnp.bfloat16), "tensor").astype(jnp.float32)
    attention = (residual.astype(jnp.float32) + head_total).astype(jnp.bfloat16)
    normed = root_norm(attention.astype(jnp.float32), norm_gain)
    attention_rows = lax.dynamic_slice_in_dim(attention, tensor_index * token_rows, token_rows, 0)
    routed_here = routes % per_owner == local_expert
    owner_index = routes // per_owner
    owner_ids = jnp.arange(expert_count, dtype=jnp.int32)
    owner_hits = jnp.sum(
        ((owner_index[:, :, None] == owner_ids[None, None, :]) & routed_here[:, :, None]).astype(
            jnp.int32
        ),
        axis=1,
    )
    rank_table = jnp.cumsum(owner_hits, axis=0) - owner_hits
    slot_index = jnp.take_along_axis(rank_table, owner_index, axis=1)
    target_owner = jnp.where(routed_here, owner_index, expert_count)
    token_ids = jnp.broadcast_to(jnp.arange(group_rows, dtype=jnp.int32)[:, None], routes.shape)
    token_table = (
        jnp.full((expert_count, capacity), group_rows, jnp.int32)
        .at[target_owner, slot_index]
        .set(token_ids, mode="drop")
    )
    gate_table = (
        jnp.zeros((expert_count, capacity), jnp.float32)
        .at[target_owner, slot_index]
        .set(gate_values, mode="drop")
    )
    padded = jnp.concatenate([normed, jnp.zeros((1, model_width), jnp.bfloat16)], axis=0)
    outgoing = jnp.take(padded, token_table.reshape(-1), axis=0).reshape(
        expert_count, capacity, model_width
    )
    slot_rows = lax.all_to_all(outgoing, "expert", split_axis=0, concat_axis=0, tiled=True)
    flat_rows = slot_rows.reshape(-1, model_width)
    gate_out = jnp.dot(flat_rows, gate_weight, preferred_element_type=jnp.float32)
    up_out = jnp.dot(flat_rows, up_weight, preferred_element_type=jnp.float32)
    activated = (jax.nn.silu(gate_out) * up_out).astype(jnp.bfloat16)
    expert_out = jnp.dot(activated, down_weight, preferred_element_type=jnp.float32).astype(
        jnp.bfloat16
    )
    returned = lax.all_to_all(
        expert_out.reshape(slot_rows.shape), "expert", split_axis=0, concat_axis=0, tiled=True
    )
    weighted = returned.reshape(-1, model_width).astype(jnp.float32) * gate_table.reshape(-1, 1)
    contribution = jax.ops.segment_sum(
        weighted, token_table.reshape(-1), num_segments=group_rows + 1
    )[:group_rows]
    expert_sum = lax.psum_scatter(
        contribution.astype(jnp.bfloat16), "tensor", scatter_dimension=0, tiled=True
    ).astype(jnp.float32)
    return (attention_rows.astype(jnp.float32) + expert_sum).astype(jnp.bfloat16)


def local(*arrays):
    expert_count, tensor_count = lax.axis_size("expert"), lax.axis_size("tensor")
    group_rows, top = arrays[4].shape
    capacity = 2 * (group_rows * top * 5 // (8 * expert_count))
    dense = (
        tensor_count == HALVES
        and expert_count % PLANE == 0
        and group_rows // tensor_count <= capacity
    )
    return (dense_local if dense else routed_local)(*arrays)


def solution(mesh):
    in_specs = (
        P("expert", "tensor"),
        P("tensor", None),
        P("expert", None),
        P(),
        P("expert", None),
        P("expert", None),
        P(None, ("expert", "tensor")),
        P(None, ("expert", "tensor")),
        P(("expert", "tensor"), None),
    )
    out_specs = P(("expert", "tensor"), None)
    return jax.shard_map(local, mesh=mesh, in_specs=in_specs, out_specs=out_specs, check_vma=False)
```

```python
import functools

import jax
import jax.numpy as jnp
from jax import lax
from jax.experimental import pallas as pl
from jax.experimental.pallas import tpu as pltpu
from jax.sharding import PartitionSpec as P


HALVES = 2
PLANE = 4
LANES = 128
AXES = ("expert", "tensor")
VMEM = pl.BlockSpec(memory_space=pltpu.VMEM)
HBM = pl.BlockSpec(memory_space=pltpu.HBM)
KERNEL_VMEM = 12 * 1024 * 1024


def head_kernel(context_hbm, weight_ref, mine_ref, other_ref, context_ref, buffer, sems):
    steps = sems.shape[0] - 1
    fetch = pltpu.make_async_copy(context_hbm, context_ref, sems.at[steps])
    fetch.start()
    depth = weight_ref.shape[0] // steps
    copies = [
        pltpu.make_async_copy(
            weight_ref.at[pl.ds(i * depth, depth), :],
            buffer.at[pl.ds(i * depth, depth), :],
            sems.at[i],
        )
        for i in range(steps)
    ]
    for copy in copies:
        copy.start()
    fetch.wait()
    total = None
    for i, copy in enumerate(copies):
        copy.wait()
        part = jnp.dot(
            context_ref[:, i * depth : (i + 1) * depth],
            buffer[i * depth : (i + 1) * depth, :],
            preferred_element_type=jnp.float32,
        )
        total = part if total is None else total + part
    rows = mine_ref.shape[0]
    low, high = total[:rows].astype(jnp.bfloat16), total[rows:].astype(jnp.bfloat16)
    first = lax.axis_index("tensor") == 0
    mine_ref[...] = jnp.where(first, low, high)
    other_ref[...] = jnp.where(first, high, low)


def head_parts(context, output_weight):
    rows = context.shape[0] // 2
    width = output_weight.shape[1]
    part = pltpu.VMEM((rows, width), jnp.bfloat16)
    steps = 16
    return pl.pallas_call(
        head_kernel,
        out_shape=(part, part),
        in_specs=[HBM, HBM],
        out_specs=(VMEM, VMEM),
        scratch_shapes=[
            pltpu.VMEM(context.shape, jnp.bfloat16),
            pltpu.VMEM(output_weight.shape, jnp.bfloat16),
            pltpu.SemaphoreType.DMA((steps + 1,)),
        ],
        compiler_params=pltpu.CompilerParams(vmem_limit_bytes=KERNEL_VMEM),
        cost_estimate=pl.CostEstimate(
            flops=2 * context.size * width,
            bytes_accessed=output_weight.size * 2,
            transcendentals=0,
        ),
        name="head_parts",
    )(*[pltpu.with_memory_space_constraint(a, pltpu.HBM) for a in (context, output_weight)])


def norm_kernel(
    experts, mine_ref, theirs_ref, residual_ref, gain_ref, routes_ref, gates_ref,
    attention_ref, block_ref,
):
    rows, width = mine_ref.shape
    start = pl.multiple_of(lax.axis_index("tensor") * rows, rows)
    head = mine_ref[...].astype(jnp.float32) + theirs_ref[...].astype(jnp.float32)
    residual = residual_ref[pl.ds(start, rows), :].astype(jnp.float32)
    attention = (residual + head).astype(jnp.bfloat16)
    attention_ref[...] = attention
    values = attention.astype(jnp.float32)
    inverse = lax.rsqrt(jnp.mean(values * values, axis=-1, keepdims=True) + 1e-06)
    block_ref[:, :width] = (values * inverse * gain_ref[...]).astype(jnp.bfloat16)
    lanes = block_ref.shape[1] - width
    lane = lax.broadcasted_iota(jnp.int32, (rows, lanes), 1)
    owner = jnp.where(lane < experts, lane, lane - experts)
    routes = routes_ref[pl.ds(start, rows), :]
    gates = gates_ref[pl.ds(start, rows), :]
    table = jnp.zeros((rows, lanes), jnp.float32)
    for k in range(routes.shape[1]):
        table = jnp.where(routes[:, k : k + 1] == owner, gates[:, k : k + 1], table)
    coarse = table.astype(jnp.bfloat16).astype(jnp.float32)
    table = jnp.where(lane < experts, coarse, table - coarse)
    block_ref[:, width:] = jnp.where(lane < 2 * experts, table, 0.0).astype(jnp.bfloat16)


def norm_block(experts, mine, theirs, residual, norm_gain, routes, gate_values):
    rows, width = mine.shape
    lanes = -(-2 * experts // LANES) * LANES
    return pl.pallas_call(
        functools.partial(norm_kernel, experts),
        out_shape=(
            pltpu.VMEM((rows, width), jnp.bfloat16),
            pltpu.VMEM((rows, width + lanes), jnp.bfloat16),
        ),
        in_specs=[VMEM] * 6,
        out_specs=(VMEM, VMEM),
        compiler_params=pltpu.CompilerParams(vmem_limit_bytes=KERNEL_VMEM),
        cost_estimate=pl.CostEstimate(
            flops=8 * mine.size, bytes_accessed=mine.size * 12, transcendentals=0
        ),
        name="norm_block",
    )(mine, theirs, residual, norm_gain.reshape(1, -1), routes, gate_values)


def stage_kernel(*refs):
    *shares, in_ref, down_ref, sems = refs
    half, _ = shares[-1].shape
    targets = [in_ref.at[:, pl.ds(i * half, half)] for i in range(4)]
    targets += [down_ref.at[pl.ds(i * half, half), :] for i in range(2)]
    copies = [
        pltpu.make_async_copy(share, target, sems.at[i])
        for i, (share, target) in enumerate(zip(shares, targets))
    ]
    for copy in copies:
        copy.start()
    for copy in copies:
        copy.wait()


def stage_weights(shares):
    half, width = shares[-1].shape
    return pl.pallas_call(
        stage_kernel,
        out_shape=(
            pltpu.VMEM((width, 4 * half), jnp.bfloat16),
            pltpu.VMEM((2 * half, width), jnp.bfloat16),
        ),
        in_specs=[HBM] * len(shares),
        out_specs=(VMEM, VMEM),
        scratch_shapes=[pltpu.SemaphoreType.DMA((len(shares),))],
        compiler_params=pltpu.CompilerParams(vmem_limit_bytes=KERNEL_VMEM),
        cost_estimate=pl.CostEstimate(
            flops=0, bytes_accessed=2 * sum(w.size for w in shares), transcendentals=0
        ),
        name="stage_weights",
    )(*[pltpu.with_memory_space_constraint(w, pltpu.HBM) for w in shares])


def expert_kernel(experts, near_ref, far_ref, in_ref, down_ref, keep_ref, send_ref):
    width, columns = in_ref.shape
    blocks = jnp.concatenate([near_ref[...], far_ref[...]], axis=0)
    table = blocks[:, width:].astype(jnp.float32)
    lane = lax.broadcasted_iota(jnp.int32, table.shape, 1)
    me = lax.axis_index("expert")
    chosen = (lane == me) | (lane == me + experts)
    weight = jnp.sum(jnp.where(chosen, table, 0.0), axis=1, keepdims=True)
    hidden = jnp.dot(blocks[:, :width], in_ref[...], preferred_element_type=jnp.float32)
    gate, up = hidden[:, : columns // 2], hidden[:, columns // 2 :]
    act = (jax.nn.silu(gate) * up * weight).astype(jnp.bfloat16)
    near_rows = near_ref.shape[0]
    step = 4 * LANES
    for j in range(width // step):
        cols = slice(j * step, (j + 1) * step)
        out = jnp.dot(act, down_ref[:, cols], preferred_element_type=jnp.float32)
        out = out.astype(jnp.bfloat16)
        keep_ref[:, cols] = out[:near_rows]
        send_ref[:, cols] = out[near_rows:]


def expert_rows(experts, near, far, weights):
    width = weights[0].shape[0]
    rows = near.shape[0] + far.shape[0]
    flops = 2 * rows * sum(w.size for w in weights)
    moved = 2 * sum(a.size for a in (*weights, near, far)) + 2 * rows * width
    return pl.pallas_call(
        functools.partial(expert_kernel, experts),
        out_shape=tuple(pltpu.VMEM((a.shape[0], width), jnp.bfloat16) for a in (near, far)),
        in_specs=[VMEM] * 4,
        out_specs=(VMEM, VMEM),
        compiler_params=pltpu.CompilerParams(vmem_limit_bytes=KERNEL_VMEM),
        cost_estimate=pl.CostEstimate(
            flops=flops, bytes_accessed=moved, transcendentals=rows * weights[0].shape[1]
        ),
        name="expert_rows",
    )(near, far, *weights)


def device_moves(expert_count, tensor_count, target):
    return [
        (e * tensor_count + t, f * tensor_count + u)
        for e in range(expert_count)
        for t in range(tensor_count)
        for f, u in [target(e, t)]
    ]


def dense_local(
    context, output_weight, residual, norm_gain, routes, gate_values, gate_weight, up_weight,
    down_weight,
):
    expert_count, tensor_count = lax.axis_size("expert"), lax.axis_size("tensor")
    rows = context.shape[0] // tensor_count

    def move(values, target):
        return lax.ppermute(values, AXES, device_moves(expert_count, tensor_count, target))

    def across(values):
        return move(values, lambda e, t: (e, 1 - t))

    def side(values):
        return move(values, lambda e, t: (e ^ (1 + t), t))

    def cross(values):
        return move(values, lambda e, t: (e ^ (2 - t), t))

    def along(values, k):
        return move(values, lambda e, t: (e ^ (k * PLANE), t))

    mine, other = head_parts(context, output_weight)
    theirs = across(other)
    shares, _ = lax.optimization_barrier(((gate_weight, up_weight, down_weight), other))
    shares = [w for share in shares for w in (share, across(share))]
    attention, block = norm_block(
        expert_count, mine, theirs, residual, norm_gain, routes, gate_values
    )
    weights = stage_weights(shares)
    blocks = [block, along(block, 1), None, along(block, 3)]
    blocks[2] = along(blocks[3], 1)
    parts = {}
    for k in (0, 1, 3, 2):
        aside = side(blocks[k])
        near = jnp.concatenate([blocks[k], aside], axis=0)
        far = cross(near)
        keep, send = expert_rows(expert_count, near, far, weights)
        added = cross(send)
        kept = keep.astype(jnp.float32) + added.astype(jnp.float32)
        passed = kept[rows:].astype(jnp.bfloat16)
        added = side(passed)
        parts[k] = kept[:rows] + added.astype(jnp.float32)
        if k == 2:
            parts[k] = parts[k] + passed_back.astype(jnp.float32)
        sent = parts[k].astype(jnp.bfloat16)
        if k == 3:
            passed_back = along(sent, 1)
        elif k:
            parts[k] = along(sent, k).astype(jnp.float32)
    total = attention.astype(jnp.float32) + (parts[0] + parts[1]) + parts[2]
    return total.astype(jnp.bfloat16)


def root_norm(values, norm_gain):
    squares = values * values
    inverse = lax.rsqrt(jnp.mean(squares, axis=-1, keepdims=True) + 1e-06)
    return (values * inverse * norm_gain).astype(jnp.bfloat16)


def routed_local(
    context,
    output_weight,
    residual,
    norm_gain,
    routes,
    gate_values,
    gate_weight,
    up_weight,
    down_weight,
):
    tensor_count = lax.axis_size("tensor")
    expert_count = lax.axis_size("expert")
    tensor_index = lax.axis_index("tensor")
    group_rows = context.shape[0]
    token_rows = group_rows // tensor_count
    model_width = residual.shape[1]
    per_owner = tensor_count // HALVES
    experts_total = expert_count * per_owner
    capacity = 2 * (group_rows * routes.shape[1] * 5 // (8 * experts_total))
    local_expert = tensor_index // HALVES
    head_part = jnp.dot(context, output_weight, preferred_element_type=jnp.float32)
    head_total = lax.psum(head_part.astype(jnp.bfloat16), "tensor").astype(jnp.float32)
    attention = (residual.astype(jnp.float32) + head_total).astype(jnp.bfloat16)
    normed = root_norm(attention.astype(jnp.float32), norm_gain)
    attention_rows = lax.dynamic_slice_in_dim(attention, tensor_index * token_rows, token_rows, 0)
    routed_here = routes % per_owner == local_expert
    owner_index = routes // per_owner
    owner_ids = jnp.arange(expert_count, dtype=jnp.int32)
    owner_hits = jnp.sum(
        ((owner_index[:, :, None] == owner_ids[None, None, :]) & routed_here[:, :, None]).astype(
            jnp.int32
        ),
        axis=1,
    )
    rank_table = jnp.cumsum(owner_hits, axis=0) - owner_hits
    slot_index = jnp.take_along_axis(rank_table, owner_index, axis=1)
    target_owner = jnp.where(routed_here, owner_index, expert_count)
    token_ids = jnp.broadcast_to(jnp.arange(group_rows, dtype=jnp.int32)[:, None], routes.shape)
    token_table = (
        jnp.full((expert_count, capacity), group_rows, jnp.int32)
        .at[target_owner, slot_index]
        .set(token_ids, mode="drop")
    )
    gate_table = (
        jnp.zeros((expert_count, capacity), jnp.float32)
        .at[target_owner, slot_index]
        .set(gate_values, mode="drop")
    )
    padded = jnp.concatenate([normed, jnp.zeros((1, model_width), jnp.bfloat16)], axis=0)
    outgoing = jnp.take(padded, token_table.reshape(-1), axis=0).reshape(
        expert_count, capacity, model_width
    )
    slot_rows = lax.all_to_all(outgoing, "expert", split_axis=0, concat_axis=0, tiled=True)
    flat_rows = slot_rows.reshape(-1, model_width)
    gate_out = jnp.dot(flat_rows, gate_weight, preferred_element_type=jnp.float32)
    up_out = jnp.dot(flat_rows, up_weight, preferred_element_type=jnp.float32)
    activated = (jax.nn.silu(gate_out) * up_out).astype(jnp.bfloat16)
    expert_out = jnp.dot(activated, down_weight, preferred_element_type=jnp.float32).astype(
        jnp.bfloat16
    )
    returned = lax.all_to_all(
        expert_out.reshape(slot_rows.shape), "expert", split_axis=0, concat_axis=0, tiled=True
    )
    weighted = returned.reshape(-1, model_width).astype(jnp.float32) * gate_table.reshape(-1, 1)
    contribution = jax.ops.segment_sum(
        weighted, token_table.reshape(-1), num_segments=group_rows + 1
    )[:group_rows]
    expert_sum = lax.psum_scatter(
        contribution.astype(jnp.bfloat16), "tensor", scatter_dimension=0, tiled=True
    ).astype(jnp.float32)
    return (attention_rows.astype(jnp.float32) + expert_sum).astype(jnp.bfloat16)


def local(*arrays):
    expert_count, tensor_count = lax.axis_size("expert"), lax.axis_size("tensor")
    group_rows, top = arrays[4].shape
    capacity = 2 * (group_rows * top * 5 // (8 * expert_count))
    dense = (
        tensor_count == HALVES
        and expert_count == PLANE * PLANE
        and group_rows // tensor_count <= capacity
    )
    return (dense_local if dense else routed_local)(*arrays)


def solution(mesh):
    in_specs = (
        P("expert", "tensor"),
        P("tensor", None),
        P("expert", None),
        P(),
        P("expert", None),
        P("expert", None),
        P(None, ("expert", "tensor")),
        P(None, ("expert", "tensor")),
        P(("expert", "tensor"), None),
    )
    out_specs = P(("expert", "tensor"), None)
    return jax.shard_map(
        local, mesh=mesh, in_specs=in_specs, out_specs=out_specs, check_vma=False
    )
```
